32 devices in a mesh: freq: 8 (over z, core), mode: 4 (over y, x).
Axes of the slice: x: 2, y: 2, z: 4, core: 2. Of those that a mesh axis runs over, the one named last changes fastest.
Arguments:
- sources: bfloat16 [16, 512, 2, 4096], P(None, None, None, ('freq', 'mode')), may hold values from -6 to 6
- mapping: bfloat16 [16, 2, 2048, 4096], P('freq', None, 'mode'), may hold values from -0.0625 to 0.0625
Outputs:
- pressure: bfloat16 [16, 512, 2, 2048], P(None, 'freq', None, 'mode')
The draws below stay inside these ranges and needn't reach their ends.
All inputs are finite; a program needn't handle non-finite values.
Results may differ from the reference program's by a relative error of at most 0.0006.
Values may be sent and summed in bfloat16 or wider, within the bound.
A program may use at most 128 MiB of HBM per device.

```python
import jax
import jax.numpy as jnp
from jax import lax

MODES = 4096
OBS = 2048
SNAP = 512
BINS = 16


def shard_levels(rng, shape, split, smallest, high):
    def one(dim, blocks):
        draws = jax.random.uniform(jax.random.fold_in(jax.random.fold_in(rng, 6), dim), (blocks,), jnp.float32, smallest / len(split), high / len(split))
        return jnp.repeat(jnp.exp(draws), shape[dim] // blocks).reshape((-1,) + (1,) * (len(shape) - dim - 1))

    loudness = one(*split[0])
    for cut in split[1:]:
        loudness = loudness * one(*cut)
    return loudness


def noise(rng, shape, width, reach, pieces=(), held_as=jnp.bfloat16):
    drawn = jax.random.normal(rng, shape, jnp.float32) * width
    if len(pieces) > 0:
        drawn = shard_levels(rng, shape, pieces, -0.22, 0.18) * drawn
    return jnp.clip(drawn, min=-reach, max=reach).astype(held_as)


def setup_inputs(seed: int = 0) -> dict:
    arg_keys = jax.random.split(jax.random.key(seed), 3)
    sources = noise(arg_keys[0], (BINS, SNAP, 2, MODES), 1.0, 6.0, ((3, 32),))
    mapping = noise(arg_keys[1], (BINS, 2, OBS, MODES), (2 * MODES) ** -0.5, 0.0625, ((0, 8), (2, 4)))
    return {"sources": sources, "mapping": mapping}


def map_bin(arrays):
    spectra, matrix = arrays
    spectra = spectra.astype(jnp.float32)
    matrix = matrix.astype(jnp.float32)
    high = lax.Precision.HIGHEST
    real_part = jnp.einsum('sm,om->so', spectra[:, 0], matrix[0], precision=high) - jnp.einsum('sm,om->so', spectra[:, 1], matrix[1], precision=high)
    imag_part = jnp.einsum('sm,om->so', spectra[:, 1], matrix[0], precision=high) + jnp.einsum('sm,om->so', spectra[:, 0], matrix[1], precision=high)
    return jnp.stack([real_part, imag_part], axis=1)

def reference(sources, mapping):
    field = lax.map(map_bin, (sources, mapping))
    weights = ((jnp.arange(BINS, dtype=jnp.float32) + 1.0) / BINS) ** 2
    energy = jnp.sum(weights[:, None, None, None] * field * field) / (SNAP * OBS)
    factor = jnp.sqrt(BINS / (energy + 1e-06))
    return (field * factor).astype(jnp.bfloat16)
```

```python
import functools

import jax
import jax.numpy as jnp
from jax import lax
from jax.experimental import pallas as pl
from jax.experimental.pallas import tpu as pltpu
from jax.sharding import PartitionSpec as P

MESH = pl.DeviceIdType.MESH
LANES = 128
AHEAD = 3


def plain_body(sources, mapping):
    freq_count = lax.axis_size("freq")
    mode_count = lax.axis_size("mode")
    bin_count = mapping.shape[0]
    slice_width = sources.shape[3]
    regrouped = lax.all_to_all(sources, "freq", split_axis=0, concat_axis=3, tiled=True)
    snapshots = regrouped.shape[1]
    blocked = regrouped.reshape(bin_count, snapshots, 2, 1, freq_count, slice_width)
    gathered = lax.all_gather(blocked, "mode", axis=3, tiled=True)
    complete = jnp.swapaxes(gathered, 3, 4).reshape(bin_count, snapshots, 2, -1)
    real_part = jnp.einsum(
        "bsm,bom->bso", complete[:, :, 0], mapping[:, 0], preferred_element_type=jnp.float32
    ) - jnp.einsum(
        "bsm,bom->bso", complete[:, :, 1], mapping[:, 1], preferred_element_type=jnp.float32
    )
    imag_part = jnp.einsum(
        "bsm,bom->bso", complete[:, :, 1], mapping[:, 0], preferred_element_type=jnp.float32
    ) + jnp.einsum(
        "bsm,bom->bso", complete[:, :, 0], mapping[:, 1], preferred_element_type=jnp.float32
    )
    field = jnp.stack([real_part, imag_part], axis=2)
    bins_total = bin_count * freq_count
    first_bin = lax.axis_index("freq") * bin_count
    bin_index = (first_bin + jnp.arange(bin_count, dtype=jnp.int32)).astype(jnp.float32)
    weights = ((bin_index + 1.0) / bins_total) ** 2
    local_energy = jnp.sum(weights[:, None, None, None] * field * field)
    energy = lax.psum(local_energy, ("freq", "mode"))
    energy = energy / (field.shape[1] * field.shape[3] * mode_count)
    factor = jnp.sqrt(bins_total / (energy + 1e-06))
    result = lax.all_to_all(
        (field * factor).astype(jnp.bfloat16), "freq", split_axis=1, concat_axis=0, tiled=True
    )
    return result


def kernel(
    dims, src, mapping, out, held, maps, field, ready, power, by_freq, by_mode,
    map_sem, own_sem, z_send, z_recv, x_send, x_recv, y_send, y_recv,
    fx_send, fx_recv, fy_send, fy_recv, ef_send, ef_recv, em_send, em_recv,
    o_own, o_send, o_recv,
):
    F, M, B, R, O = dims
    half = F // 2
    f = lax.axis_index("freq")
    m = lax.axis_index("mode")
    mx = m + 1 - 2 * lax.rem(m, 2)
    my = lax.rem(m + 2, 4)

    def freq_peer(step):
        return lax.rem(f + step, F)

    def mode_peer(step):
        return lax.rem(m + step, M)

    for b in range(B):
        for c in range(2):
            pltpu.make_async_copy(mapping.at[b, c], maps.at[b, c], map_sem.at[b, c]).start()

    def own_copy(k):
        return pltpu.make_async_copy(
            src.at[pl.ds(f * B, B), pl.ds(k * R, R)], held.at[k, m, f], own_sem.at[k]
        )

    def own_start(k, carry):
        own_copy(k).start()
        return carry

    lax.fori_loop(0, F, own_start, 0)

    barrier = pltpu.get_barrier_semaphore()
    for step in range(1, F):
        pl.semaphore_signal(barrier, inc=1, device_id=(freq_peer(step), m), device_id_type=MESH)
    for step in range(1, M):
        pl.semaphore_signal(barrier, inc=1, device_id=(f, mode_peer(step)), device_id_type=MESH)
    pl.semaphore_wait(barrier, F + M - 2)

    def z_start(k):
        for step in range(1, F):
            there = freq_peer(step)
            pltpu.make_async_remote_copy(
                src_ref=src.at[pl.ds(there * B, B), pl.ds(k * R, R)],
                dst_ref=held.at[k, m, f],
                send_sem=z_send.at[k],
                recv_sem=z_recv.at[k],
                device_id=(there, m),
                device_id_type=MESH,
            ).start()

    def z_wait(sem, k):
        peers = held.at[k, m, pl.ds(0, F - 1)]
        pltpu.make_async_copy(peers, peers, sem.at[k]).wait()

    def spread(k, to, send, recv):
        return pltpu.make_async_remote_copy(
            src_ref=held.at[k, m], dst_ref=held.at[k, m],
            send_sem=send.at[k], recv_sem=recv.at[k],
            device_id=(f, to), device_id_type=MESH,
        )

    def relay(k, whose, first, to, send, recv):
        part = held.at[k, whose, pl.ds(first, half)]
        return pltpu.make_async_remote_copy(
            src_ref=part, dst_ref=part,
            send_sem=send.at[k], recv_sem=recv.at[k],
            device_id=(f, to), device_id_type=MESH,
        )

    def compute(k):
        def one_bin(b, carry):
            direct = None
            for g in range(F):
                lhs = jnp.concatenate([held[k, j, g, b] for j in range(M)], axis=1)
                cols = pl.ds(g * M * LANES, M * LANES)
                nt = (((1,), (1,)), ((), ()))
                p = lax.dot_general(lhs, maps[b, 0, :, cols], nt, preferred_element_type=jnp.float32)
                q = lax.dot_general(lhs, maps[b, 1, :, cols], nt, preferred_element_type=jnp.float32)
                direct = p if direct is None else direct + p
                cross = q if g == 0 else cross + q
            even = lax.rem(lax.broadcasted_iota(jnp.int32, (R, O), 0), 2) == 0
            turned = jnp.where(even, -pltpu.roll(cross, R - 1, 0), pltpu.roll(cross, 1, 0))
            value = direct + turned
            field[k, b] = value
            root = (f * B + b + 1).astype(jnp.float32) / (B * F)
            squares = jnp.sum((value * value).reshape(R // 8, 8, O), axis=0)
            folded = squares[:, :LANES]
            for j in range(1, O // LANES):
                folded = folded + squares[:, j * LANES : (j + 1) * LANES]
            power[...] += folded * (root * root)
            return carry

        lax.fori_loop(0, B, one_bin, 0)

    power[...] = jnp.zeros_like(power)
    for k in range(min(AHEAD, F)):
        z_start(k)

    def step_fn(k, carry):
        @pl.when(k < F)
        def _():
            own_copy(k).wait()
            z_wait(z_recv, k)
            spread(k, mx, x_send, x_recv).start()
            spread(k, my, y_send, y_recv).start()

        @pl.when(k + AHEAD < F)
        def _():
            z_start(k + AHEAD)

        @pl.when((k >= 1) & (k <= F))
        def _():
            last = k - 1
            spread(last, mx, x_send, x_recv).wait_recv()
            relay(last, mx, 0, my, fy_send, fy_recv).start()
            spread(last, my, y_send, y_recv).wait_recv()
            relay(last, my, half, mx, fx_send, fx_recv).start()

        @pl.when(k == 2)
        def _():
            for b in range(B):
                for c in range(2):
                    pltpu.make_async_copy(mapping.at[b, c], maps.at[b, c], map_sem.at[b, c]).wait()

        @pl.when(k >= 2)
        def _():
            done = k - 2
            relay(done, mx, 0, my, fy_send, fy_recv).wait_recv()
            relay(done, my, half, mx, fx_send, fx_recv).wait_recv()
            compute(done)

        return carry

    lax.fori_loop(0, F + 2, step_fn, 0)

    by_freq[f] = power[...]
    for step in range(1, F):
        pltpu.make_async_remote_copy(
            src_ref=power, dst_ref=by_freq.at[f], send_sem=ef_send, recv_sem=ef_recv,
            device_id=(freq_peer(step), m), device_id_type=MESH,
        ).start()
    peers = by_freq.at[pl.ds(0, F - 1)]
    pltpu.make_async_copy(peers, peers, ef_recv).wait()
    pltpu.make_async_copy(peers, peers, ef_send).wait()
    power[...] = jnp.sum(by_freq[...], axis=0)
    by_mode[m] = power[...]
    for step in range(1, M):
        pltpu.make_async_remote_copy(
            src_ref=power, dst_ref=by_mode.at[m], send_sem=em_send, recv_sem=em_recv,
            device_id=(f, mode_peer(step)), device_id_type=MESH,
        ).start()
    peers = by_mode.at[pl.ds(0, M - 1)]
    pltpu.make_async_copy(peers, peers, em_recv).wait()
    pltpu.make_async_copy(peers, peers, em_send).wait()
    energy = jnp.sum(jnp.sum(by_mode[...], axis=0), keepdims=True) / (F * (R // 2) * O * M)
    factor = jnp.sqrt(B * F / (energy + 1e-06))

    def scale(k):
        for b in range(B):
            for j in range(O // LANES):
                piece = field[k, b, :, j * LANES : (j + 1) * LANES] * factor
                ready[k, b, j] = piece.astype(jnp.bfloat16)

    def finish(step, carry):
        there = freq_peer(step)
        scale(there)
        pltpu.make_async_remote_copy(
            src_ref=ready.at[there], dst_ref=out.at[pl.ds(f * B, B)],
            send_sem=o_send, recv_sem=o_recv,
            device_id=(there, m), device_id_type=MESH,
        ).start()
        return carry

    lax.fori_loop(1, F, finish, 0)
    scale(f)
    mine = pltpu.make_async_copy(ready.at[f], out.at[pl.ds(f * B, B)], o_own)
    mine.start()

    def drain(k, carry):
        z_wait(z_send, k)
        spread(k, mx, x_send, x_recv).wait_send()
        spread(k, my, y_send, y_recv).wait_send()
        relay(k, mx, 0, my, fy_send, fy_recv).wait_send()
        relay(k, my, half, mx, fx_send, fx_recv).wait_send()
        return carry

    lax.fori_loop(0, F, drain, 0)
    mine.wait()
    peers = ready.at[pl.ds(0, F - 1)]
    pltpu.make_async_copy(peers, peers, o_send).wait()
    pltpu.make_async_copy(peers, peers, o_recv).wait()


def kernel_body(sources, mapping):
    F = lax.axis_size("freq")
    M = lax.axis_size("mode")
    bins, snaps = sources.shape[:2]
    B, _, O, modes = mapping.shape
    R = 2 * snaps // F
    dma = pltpu.SemaphoreType.DMA
    any_space = pl.BlockSpec(memory_space=pl.ANY)
    out = pl.pallas_call(
        functools.partial(kernel, (F, M, B, R, O)),
        out_shape=jax.ShapeDtypeStruct((bins, O // LANES, R, LANES), jnp.bfloat16),
        in_specs=[any_space, any_space],
        out_specs=any_space,
        scratch_shapes=[
            pltpu.VMEM((F, M, F, B, R, LANES), jnp.bfloat16),
            pltpu.VMEM((B, 2, O, modes), jnp.bfloat16),
            pltpu.VMEM((F, B, R, O), jnp.float32),
            pltpu.VMEM((F, B, O // LANES, R, LANES), jnp.bfloat16),
            pltpu.VMEM((8, LANES), jnp.float32),
            pltpu.VMEM((F, 8, LANES), jnp.float32),
            pltpu.VMEM((M, 8, LANES), jnp.float32),
            dma((B, 2)),
            dma((F,)),
        ]
        + [dma((F,))] * 10
        + [dma(())] * 7,
        compiler_params=pltpu.CompilerParams(
            collective_id=0, has_side_effects=True, vmem_limit_bytes=62 * 1024 * 1024
        ),
    )(sources.reshape(bins, 2 * snaps, LANES), mapping)
    out = out.reshape(bins, O // LANES, R // 2, 2, LANES)
    return jnp.transpose(out, (0, 2, 3, 1, 4)).reshape(bins, R // 2, 2, O)


def body(sources, mapping):
    freq_count = lax.axis_size("freq")
    snaps, width = sources.shape[1], sources.shape[3]
    held = 2 * mapping.size + 2 * mapping.shape[0] * snaps * 2 * mapping.shape[3]
    fits = (
        lax.axis_size("mode") == 4
        and freq_count % 2 == 0
        and width == LANES
        and mapping.shape[2] % LANES == 0
        and snaps % (8 * freq_count) == 0
        and held <= 40 * 1024 * 1024
    )
    return (kernel_body if fits else plain_body)(sources, mapping)


def solution(mesh):
    placed = (P(None, None, None, ("freq", "mode")), P("freq", None, "mode", None))
    return jax.shard_map(
        body, mesh=mesh, in_specs=placed, out_specs=P(None, "freq", None, "mode"), check_vma=False
    )
```

```python
import functools

import jax
import jax.numpy as jnp
from jax import lax
from jax.experimental import pallas as pl
from jax.experimental.pallas import tpu as pltpu
from jax.sharding import PartitionSpec as P

MESH = pl.DeviceIdType.MESH
LANES = 128
AHEAD = 3
ROWS = 16
EARLY = 5


def plain_body(sources, mapping):
    freq_count = lax.axis_size("freq")
    mode_count = lax.axis_size("mode")
    bin_count = mapping.shape[0]
    slice_width = sources.shape[3]
    regrouped = lax.all_to_all(sources, "freq", split_axis=0, concat_axis=3, tiled=True)
    snapshots = regrouped.shape[1]
    blocked = regrouped.reshape(bin_count, snapshots, 2, 1, freq_count, slice_width)
    gathered = lax.all_gather(blocked, "mode", axis=3, tiled=True)
    complete = jnp.swapaxes(gathered, 3, 4).reshape(bin_count, snapshots, 2, -1)
    real_part = jnp.einsum(
        "bsm,bom->bso", complete[:, :, 0], mapping[:, 0], preferred_element_type=jnp.float32
    ) - jnp.einsum(
        "bsm,bom->bso", complete[:, :, 1], mapping[:, 1], preferred_element_type=jnp.float32
    )
    imag_part = jnp.einsum(
        "bsm,bom->bso", complete[:, :, 1], mapping[:, 0], preferred_element_type=jnp.float32
    ) + jnp.einsum(
        "bsm,bom->bso", complete[:, :, 0], mapping[:, 1], preferred_element_type=jnp.float32
    )
    field = jnp.stack([real_part, imag_part], axis=2)
    bins_total = bin_count * freq_count
    first_bin = lax.axis_index("freq") * bin_count
    bin_index = (first_bin + jnp.arange(bin_count, dtype=jnp.int32)).astype(jnp.float32)
    weights = ((bin_index + 1.0) / bins_total) ** 2
    local_energy = jnp.sum(weights[:, None, None, None] * field * field)
    energy = lax.psum(local_energy, ("freq", "mode"))
    energy = energy / (field.shape[1] * field.shape[3] * mode_count)
    factor = jnp.sqrt(bins_total / (energy + 1e-06))
    result = lax.all_to_all(
        (field * factor).astype(jnp.bfloat16), "freq", split_axis=1, concat_axis=0, tiled=True
    )
    return result


def kernel(
    dims, src, mapping, out, held, maps, field, early, ready, scaled, power, by_mode, by_freq,
    map_sem, own_sem, z_send, z_recv, x_send, x_recv, y_send, y_recv,
    fx_send, fx_recv, fy_send, fy_recv, e_send, e_recv,
    ox_send, ox_recv, oy_send, oy_recv, of_send, of_recv,
    em_send, em_recv, ef_send, ef_recv, o_own, o_send, o_recv,
):
    F, M, B, K, C, O, E = dims
    R = F * C
    cut = F // 2
    f = lax.axis_index("freq")
    m = lax.axis_index("mode")
    mx = m + 1 - 2 * lax.rem(m, 2)
    my = lax.rem(m + 2, 4)
    md = lax.rem(mx + 2, 4)

    def freq_peer(step):
        return lax.rem(f + step, F)

    def mode_peer(step):
        return lax.rem(m + step, M)

    def remote(src_ref, dst_ref, send, recv, to_f, to_m):
        return pltpu.make_async_remote_copy(
            src_ref=src_ref, dst_ref=dst_ref, send_sem=send, recv_sem=recv,
            device_id=(to_f, to_m), device_id_type=MESH,
        )

    def await_bytes(ref, sem):
        pltpu.make_async_copy(ref, ref, sem).wait()

    def chunk(owner, k):
        return src.at[pl.ds(owner * B, B), :, pl.ds(pl.multiple_of(k * C, C), C)]

    def own_copy(k):
        return pltpu.make_async_copy(chunk(f, k), held.at[k, m, 0], own_sem.at[k])

    barrier = pltpu.get_barrier_semaphore()
    for step in range(1, F):
        pl.semaphore_signal(barrier, inc=1, device_id=(freq_peer(step), m), device_id_type=MESH)
    for step in range(1, M):
        pl.semaphore_signal(barrier, inc=1, device_id=(f, mode_peer(step)), device_id_type=MESH)
    pl.semaphore_wait(barrier, F + M - 2)

    def z_start(k):
        for step in range(1, F):
            there = freq_peer(step)
            remote(
                chunk(there, k), held.at[k, m, F - step], z_send.at[k], z_recv.at[k], there, m
            ).start()

    def z_slots(k):
        return held.at[k, m, pl.ds(1, F - 1)]

    def spread(k, whose, to, send, recv):
        part = held.at[k, whose, pl.ds(1, F - 1)]
        return remote(part, part, send.at[k], recv.at[k], f, to)

    def relay_y(k):
        part = held.at[k, mx, pl.ds(1, cut - 1)]
        return remote(part, part, fy_send.at[k], fy_recv.at[k], f, my)

    def relay_x(k):
        part = held.at[k, my, pl.ds(cut, F - cut)]
        return remote(part, part, fx_send.at[k], fx_recv.at[k], f, mx)

    def own_slots(whose):
        return held.at[pl.ds(0, K), whose, 0]

    def own_relay():
        return remote(own_slots(mx), own_slots(mx), of_send, of_recv, f, my)

    def partial_field(k, b, whose):
        direct = cross = None
        nt = (((1,), (1,)), ((), ()))
        for w in whose:
            lhs = jnp.concatenate([held[k, w, r, b].reshape(R, LANES) for r in range(F)], axis=1)
            starts = [
                pl.multiple_of((lax.rem(f + r, F) * M + w) * LANES, LANES) for r in range(F)
            ]
            for c in range(2):
                rhs = jnp.concatenate([maps[b, c, :, pl.ds(s, LANES)] for s in starts], axis=1)
                term = lax.dot_general(lhs, rhs, nt, preferred_element_type=jnp.float32)
                if c == 0:
                    direct = term if direct is None else direct + term
                else:
                    cross = term if cross is None else cross + term
        even = lax.rem(lax.broadcasted_iota(jnp.int32, (R, O), 0), 2) == 0
        turned = jnp.where(even, -pltpu.roll(cross, R - 1, 0), pltpu.roll(cross, 1, 0))
        return direct + turned

    def near_part(k):
        def one_bin(b, carry):
            field[k, b] = partial_field(k, b, (m, mx, my)).reshape(F, C, O)
            return carry

        lax.fori_loop(0, B, one_bin, 0)

    def far_part(k):
        def one_bin(b, carry):
            value = field[k, b].reshape(R, O) + partial_field(k, b, (md,))
            field[k, b] = value.reshape(F, C, O)
            root = (f * B + b + 1).astype(jnp.float32) / (B * F)
            squares = jnp.sum((value * value).reshape(R // 8, 8, O), axis=0)
            folded = squares[:, :LANES]
            for j in range(1, O // LANES):
                folded = folded + squares[:, j * LANES : (j + 1) * LANES]
            power[...] += folded * (root * root)
            return carry

        lax.fori_loop(0, B, one_bin, 0)

    def early_start(k):
        early[f, k] = field[k, :, f]
        for step in range(1, F):
            there = freq_peer(step)
            remote(
                field.at[k, :, there], early.at[f, k], e_send.at[k], e_recv.at[k], there, m
            ).start()

    def early_slots(k):
        return early.at[pl.ds(0, F - 1), k]

    z_start(0)

    def own_start(k, carry):
        remote(chunk(f, k), held.at[k, m, 0], ox_send, ox_recv, f, mx).start()
        remote(chunk(f, k), held.at[k, m, 0], oy_send, oy_recv, f, my).start()
        own_copy(k).start()
        return carry

    lax.fori_loop(0, K, own_start, 0)
    for k in range(1, min(AHEAD, K)):
        z_start(k)
    for b in range(B):
        for c in range(2):
            pltpu.make_async_copy(mapping.at[b, c], maps.at[b, c], map_sem.at[b, c]).start()
    power[...] = jnp.zeros_like(power)

    def step_fn(k, carry):
        @pl.when(k < K)
        def _():
            await_bytes(z_slots(k), z_recv.at[k])
            spread(k, m, mx, x_send, x_recv).start()
            spread(k, m, my, y_send, y_recv).start()
            own_copy(k).wait()

        @pl.when(k + AHEAD < K)
        def _():
            z_start(k + AHEAD)

        @pl.when(k == 0)
        def _():
            await_bytes(own_slots(mx), ox_recv)
            own_relay().start()
            await_bytes(own_slots(my), oy_recv)
            for b in range(B):
                for c in range(2):
                    pltpu.make_async_copy(mapping.at[b, c], maps.at[b, c], map_sem.at[b, c]).wait()

        @pl.when((k >= 1) & (k <= K))
        def _():
            last = k - 1
            spread(last, mx, mx, x_send, x_recv).wait_recv()
            relay_y(last).start()
            spread(last, my, my, y_send, y_recv).wait_recv()
            relay_x(last).start()
            near_part(last)

        @pl.when(k == 2)
        def _():
            own_relay().wait_recv()

        @pl.when(k >= 2)
        def _():
            done = k - 2
            relay_y(done).wait_recv()
            relay_x(done).wait_recv()
            far_part(done)

            @pl.when(done < E)
            def _():
                early_start(done)

        return carry

    lax.fori_loop(0, K + 2, step_fn, 0)

    by_mode[m] = power[...]
    for step in range(1, M):
        remote(power, by_mode.at[m], em_send, em_recv, f, mode_peer(step)).start()
    await_bytes(by_mode.at[pl.ds(0, M - 1)], em_recv)
    await_bytes(by_mode.at[pl.ds(0, M - 1)], em_send)
    power[...] = jnp.sum(by_mode[...], axis=0)
    by_freq[f] = power[...]
    for step in range(1, F):
        remote(power, by_freq.at[f], ef_send, ef_recv, freq_peer(step), m).start()
    await_bytes(by_freq.at[pl.ds(0, F - 1)], ef_recv)
    await_bytes(by_freq.at[pl.ds(0, F - 1)], ef_send)
    count = F * K * C // 2 * O * M
    energy = jnp.sum(jnp.sum(by_freq[...], axis=0), keepdims=True) / count
    factor = jnp.sqrt(B * F / (energy + 1e-06))
    blocks = O // LANES

    def scale_late(d):
        for k in range(E, K):
            for b in range(B):
                value = (field[k, b, d] * factor).astype(jnp.bfloat16)
                for j in range(blocks):
                    ready[d, b, j, (k - E) * C : (k - E + 1) * C] = value[:, j * LANES : (j + 1) * LANES]

    def late_rows():
        return out.at[pl.ds(f * B, B), :, pl.ds(E * C, (K - E) * C)]

    def late_start(step, carry):
        there = freq_peer(step)
        scale_late(there)
        remote(ready.at[there], late_rows(), o_send, o_recv, there, m).start()
        return carry

    lax.fori_loop(1, F, late_start, 0)
    scale_late(f)
    mine = pltpu.make_async_copy(ready.at[f], late_rows(), o_own.at[0])
    mine.start()

    def early_wait(k, carry):
        await_bytes(early_slots(k), e_recv.at[k])
        return carry

    lax.fori_loop(0, E, early_wait, 0)

    def scale_early(s, carry):
        for k in range(E):
            for b in range(B):
                value = (early[s, k, b] * factor).astype(jnp.bfloat16)
                for j in range(blocks):
                    scaled[s * B + b, j, k * C : (k + 1) * C] = value[:, j * LANES : (j + 1) * LANES]
        return carry

    lax.fori_loop(0, F, scale_early, 0)
    first = pltpu.make_async_copy(scaled, out.at[:, :, pl.ds(0, E * C)], o_own.at[1])
    first.start()

    def drain(k, carry):
        await_bytes(z_slots(k), z_send.at[k])
        spread(k, m, mx, x_send, x_recv).wait_send()
        spread(k, m, my, y_send, y_recv).wait_send()
        relay_y(k).wait_send()
        relay_x(k).wait_send()

        @pl.when(k < E)
        def _():
            await_bytes(early_slots(k), e_send.at[k])

        return carry

    lax.fori_loop(0, K, drain, 0)
    await_bytes(own_slots(m), ox_send)
    await_bytes(own_slots(m), oy_send)
    own_relay().wait_send()
    mine.wait()
    first.wait()
    await_bytes(ready.at[pl.ds(0, F - 1)], o_send)
    await_bytes(ready.at[pl.ds(0, F - 1)], o_recv)


def kernel_body(sources, mapping):
    F = lax.axis_size("freq")
    M = lax.axis_size("mode")
    bins, snaps = sources.shape[:2]
    B, _, O, modes = mapping.shape
    rows = 2 * snaps // F
    C = ROWS
    K = rows // C
    E = K * EARLY // 8
    blocks = O // LANES
    dma = pltpu.SemaphoreType.DMA
    any_space = pl.BlockSpec(memory_space=pl.ANY)
    out = pl.pallas_call(
        functools.partial(kernel, (F, M, B, K, C, O, E)),
        out_shape=jax.ShapeDtypeStruct((bins, blocks, rows, LANES), jnp.bfloat16),
        in_specs=[any_space, any_space],
        out_specs=any_space,
        scratch_shapes=[
            pltpu.VMEM((K, M, F, B, F, C, LANES), jnp.bfloat16),
            pltpu.VMEM((B, 2, O, modes), jnp.bfloat16),
            pltpu.VMEM((K, B, F, C, O), jnp.float32),
            pltpu.VMEM((F, E, B, C, O), jnp.float32),
            pltpu.VMEM((F, B, blocks, (K - E) * C, LANES), jnp.bfloat16),
            pltpu.VMEM((bins, blocks, E * C, LANES), jnp.bfloat16),
            pltpu.VMEM((8, LANES), jnp.float32),
            pltpu.VMEM((M, 8, LANES), jnp.float32),
            pltpu.VMEM((F, 8, LANES), jnp.float32),
            dma((B, 2)),
        ]
        + [dma((K,))] * 11
        + [dma((E,))] * 2
        + [dma(())] * 10
        + [dma((2,))]
        + [dma(())] * 2,
        compiler_params=pltpu.CompilerParams(
            collective_id=0, has_side_effects=True, vmem_limit_bytes=62 * 1024 * 1024
        ),
    )(sources.reshape(bins, F, rows, LANES), mapping)
    out = out.reshape(bins, blocks, rows // 2, 2, LANES)
    return jnp.transpose(out, (0, 2, 3, 1, 4)).reshape(bins, rows // 2, 2, O)


def body(sources, mapping):
    freq_count = lax.axis_size("freq")
    snaps, width = sources.shape[1], sources.shape[3]
    held = 2 * mapping.size + 2 * mapping.shape[0] * snaps * 2 * mapping.shape[3]
    fits = (
        lax.axis_size("mode") == 4
        and freq_count % 2 == 0
        and width == LANES
        and mapping.shape[2] % LANES == 0
        and snaps % (4 * ROWS * freq_count) == 0
        and held <= 40 * 1024 * 1024
    )
    return (kernel_body if fits else plain_body)(sources, mapping)


def solution(mesh):
    placed = (P(None, None, None, ("freq", "mode")), P("freq", None, "mode", None))
    return jax.shard_map(
        body, mesh=mesh, in_specs=placed, out_specs=P(None, "freq", None, "mode"), check_vma=False
    )
```

```python
import functools

import jax
import jax.numpy as jnp
from jax import lax
from jax.experimental import pallas as pl
from jax.experimental.pallas import tpu as pltpu
from jax.sharding import PartitionSpec as P

MESH = pl.DeviceIdType.MESH
LANES = 128
AHEAD = 3
ROWS = 16
EARLY = 6


def plain_body(sources, mapping):
    freq_count = lax.axis_size("freq")
    mode_count = lax.axis_size("mode")
    bin_count = mapping.shape[0]
    slice_width = sources.shape[3]
    regrouped = lax.all_to_all(sources, "freq", split_axis=0, concat_axis=3, tiled=True)
    snapshots = regrouped.shape[1]
    blocked = regrouped.reshape(bin_count, snapshots, 2, 1, freq_count, slice_width)
    gathered = lax.all_gather(blocked, "mode", axis=3, tiled=True)
    complete = jnp.swapaxes(gathered, 3, 4).reshape(bin_count, snapshots, 2, -1)
    real_part = jnp.einsum(
        "bsm,bom->bso", complete[:, :, 0], mapping[:, 0], preferred_element_type=jnp.float32
    ) - jnp.einsum(
        "bsm,bom->bso", complete[:, :, 1], mapping[:, 1], preferred_element_type=jnp.float32
    )
    imag_part = jnp.einsum(
        "bsm,bom->bso", complete[:, :, 1], mapping[:, 0], preferred_element_type=jnp.float32
    ) + jnp.einsum(
        "bsm,bom->bso", complete[:, :, 0], mapping[:, 1], preferred_element_type=jnp.float32
    )
    field = jnp.stack([real_part, imag_part], axis=2)
    bins_total = bin_count * freq_count
    first_bin = lax.axis_index("freq") * bin_count
    bin_index = (first_bin + jnp.arange(bin_count, dtype=jnp.int32)).astype(jnp.float32)
    weights = ((bin_index + 1.0) / bins_total) ** 2
    local_energy = jnp.sum(weights[:, None, None, None] * field * field)
    energy = lax.psum(local_energy, ("freq", "mode"))
    energy = energy / (field.shape[1] * field.shape[3] * mode_count)
    factor = jnp.sqrt(bins_total / (energy + 1e-06))
    result = lax.all_to_all(
        (field * factor).astype(jnp.bfloat16), "freq", split_axis=1, concat_axis=0, tiled=True
    )
    return result


def kernel(
    dims, src, mapping, out, held, maps, field, early, ready, scaled, power, by_mode, by_freq,
    map_sem, own_sem, z_send, z_recv, x_send, x_recv, y_send, y_recv,
    fx_send, fx_recv, fy_send, fy_recv, e_send, e_recv,
    ox_send, ox_recv, oy_send, oy_recv, of_send, of_recv,
    em_send, em_recv, ef_send, ef_recv, o_own, o_send, o_recv,
):
    F, M, B, K, C, O, E = dims
    R = F * C
    cut = F // 2
    f = lax.axis_index("freq")
    m = lax.axis_index("mode")
    mx = m + 1 - 2 * lax.rem(m, 2)
    my = lax.rem(m + 2, 4)
    md = lax.rem(mx + 2, 4)

    def freq_peer(step):
        return lax.rem(f + step, F)

    def mode_peer(step):
        return lax.rem(m + step, M)

    def remote(src_ref, dst_ref, send, recv, to_f, to_m):
        return pltpu.make_async_remote_copy(
            src_ref=src_ref, dst_ref=dst_ref, send_sem=send, recv_sem=recv,
            device_id=(to_f, to_m), device_id_type=MESH,
        )

    def await_bytes(ref, sem):
        pltpu.make_async_copy(ref, ref, sem).wait()

    def chunk(owner, k):
        return src.at[pl.ds(owner * B, B), :, pl.ds(pl.multiple_of(k * C, C), C)]

    def own_copy(k):
        return pltpu.make_async_copy(chunk(f, k), held.at[k, m, 0], own_sem.at[k])

    barrier = pltpu.get_barrier_semaphore()
    for step in range(1, F):
        pl.semaphore_signal(barrier, inc=1, device_id=(freq_peer(step), m), device_id_type=MESH)
    for step in range(1, M):
        pl.semaphore_signal(barrier, inc=1, device_id=(f, mode_peer(step)), device_id_type=MESH)
    pl.semaphore_wait(barrier, F + M - 2)

    def z_start(k):
        for step in range(1, F):
            there = freq_peer(step)
            remote(
                chunk(there, k), held.at[k, m, F - step], z_send.at[k], z_recv.at[k], there, m
            ).start()

    def z_slots(k):
        return held.at[k, m, pl.ds(1, F - 1)]

    def spread(k, whose, to, send, recv):
        part = held.at[k, whose, pl.ds(1, F - 1)]
        return remote(part, part, send.at[k], recv.at[k], f, to)

    def relay_y(k):
        part = held.at[k, mx, pl.ds(1, cut - 1)]
        return remote(part, part, fy_send.at[k], fy_recv.at[k], f, my)

    def relay_x(k):
        part = held.at[k, my, pl.ds(cut, F - cut)]
        return remote(part, part, fx_send.at[k], fx_recv.at[k], f, mx)

    def own_slots(whose):
        return held.at[pl.ds(0, K), whose, 0]

    def own_relay():
        return remote(own_slots(mx), own_slots(mx), of_send, of_recv, f, my)

    def partial_field(k, b, whose):
        direct = cross = None
        nt = (((1,), (1,)), ((), ()))
        for w in whose:
            lhs = jnp.concatenate([held[k, w, r, b].reshape(R, LANES) for r in range(F)], axis=1)
            starts = [
                pl.multiple_of((lax.rem(f + r, F) * M + w) * LANES, LANES) for r in range(F)
            ]
            for c in range(2):
                rhs = jnp.concatenate([maps[b, c, :, pl.ds(s, LANES)] for s in starts], axis=1)
                term = lax.dot_general(lhs, rhs, nt, preferred_element_type=jnp.float32)
                if c == 0:
                    direct = term if direct is None else direct + term
                else:
                    cross = term if cross is None else cross + term
        even = lax.rem(lax.broadcasted_iota(jnp.int32, (R, O), 0), 2) == 0
        turned = jnp.where(even, -pltpu.roll(cross, R - 1, 0), pltpu.roll(cross, 1, 0))
        return direct + turned

    def near_part(k):
        def one_bin(b, carry):
            field[k, b] = partial_field(k, b, (m, mx, my)).reshape(F, C, O)
            return carry

        lax.fori_loop(0, B, one_bin, 0)

    def far_part(k):
        def one_bin(b, carry):
            value = field[k, b].reshape(R, O) + partial_field(k, b, (md,))
            field[k, b] = value.reshape(F, C, O)
            root = (f * B + b + 1).astype(jnp.float32) / (B * F)
            squares = jnp.sum((value * value).reshape(R // 8, 8, O), axis=0)
            folded = squares[:, :LANES]
            for j in range(1, O // LANES):
                folded = folded + squares[:, j * LANES : (j + 1) * LANES]
            power[...] += folded * (root * root)
            return carry

        lax.fori_loop(0, B, one_bin, 0)

    def early_start(k):
        early[f, k] = field[k, :, f]
        for step in range(1, F):
            there = freq_peer(step)
            remote(
                field.at[k, :, there], early.at[f, k], e_send.at[k], e_recv.at[k], there, m
            ).start()

    def early_slots(k):
        return early.at[pl.ds(0, F - 1), k]

    z_start(0)

    def own_start(k, carry):
        remote(chunk(f, k), held.at[k, m, 0], ox_send, ox_recv, f, mx).start()
        remote(chunk(f, k), held.at[k, m, 0], oy_send, oy_recv, f, my).start()
        own_copy(k).start()
        return carry

    lax.fori_loop(0, K, own_start, 0)
    for k in range(1, min(AHEAD, K)):
        z_start(k)
    for b in range(B):
        for c in range(2):
            pltpu.make_async_copy(mapping.at[b, c], maps.at[b, c], map_sem.at[b, c]).start()
    power[...] = jnp.zeros_like(power)

    def step_fn(k, carry):
        @pl.when(k < K)
        def _():
            await_bytes(z_slots(k), z_recv.at[k])
            spread(k, m, mx, x_send, x_recv).start()
            spread(k, m, my, y_send, y_recv).start()
            own_copy(k).wait()

        @pl.when(k + AHEAD < K)
        def _():
            z_start(k + AHEAD)

        @pl.when(k == 0)
        def _():
            await_bytes(own_slots(mx), ox_recv)
            own_relay().start()
            await_bytes(own_slots(my), oy_recv)
            for b in range(B):
                for c in range(2):
                    pltpu.make_async_copy(mapping.at[b, c], maps.at[b, c], map_sem.at[b, c]).wait()

        @pl.when((k >= 1) & (k <= K))
        def _():
            last = k - 1
            spread(last, mx, mx, x_send, x_recv).wait_recv()
            relay_y(last).start()
            spread(last, my, my, y_send, y_recv).wait_recv()
            relay_x(last).start()
            near_part(last)

        @pl.when(k == 2)
        def _():
            own_relay().wait_recv()

        @pl.when(k >= 2)
        def _():
            done = k - 2
            relay_y(done).wait_recv()
            relay_x(done).wait_recv()
            far_part(done)

            @pl.when(done < E)
            def _():
                early_start(done)

        return carry

    lax.fori_loop(0, K + 2, step_fn, 0)

    by_mode[m] = power[...]
    for step in range(1, M):
        remote(power, by_mode.at[m], em_send, em_recv, f, mode_peer(step)).start()
    await_bytes(by_mode.at[pl.ds(0, M - 1)], em_recv)
    await_bytes(by_mode.at[pl.ds(0, M - 1)], em_send)
    power[...] = jnp.sum(by_mode[...], axis=0)
    by_freq[f] = power[...]
    for step in range(1, F):
        remote(power, by_freq.at[f], ef_send, ef_recv, freq_peer(step), m).start()
    await_bytes(by_freq.at[pl.ds(0, F - 1)], ef_recv)
    await_bytes(by_freq.at[pl.ds(0, F - 1)], ef_send)
    count = F * K * C // 2 * O * M
    energy = jnp.sum(jnp.sum(by_freq[...], axis=0), keepdims=True) / count
    factor = jnp.sqrt(B * F / (energy + 1e-06))
    blocks = O // LANES

    def scale_late(d):
        for k in range(E, K):
            for b in range(B):
                value = (field[k, b, d] * factor).astype(jnp.bfloat16)
                for j in range(blocks):
                    ready[d, b, j, (k - E) * C : (k - E + 1) * C] = value[:, j * LANES : (j + 1) * LANES]

    def late_rows():
        return out.at[pl.ds(f * B, B), :, pl.ds(E * C, (K - E) * C)]

    def late_start(i, carry):
        step = lax.rem(cut + (1 - 2 * lax.rem(i, 2)) * ((i + 1) // 2) + F, F)
        there = freq_peer(step)
        scale_late(there)
        remote(ready.at[there], late_rows(), o_send, o_recv, there, m).start()
        return carry

    lax.fori_loop(0, F - 1, late_start, 0)
    scale_late(f)
    mine = pltpu.make_async_copy(ready.at[f], late_rows(), o_own.at[0])
    mine.start()

    def early_wait(k, carry):
        await_bytes(early_slots(k), e_recv.at[k])
        return carry

    lax.fori_loop(0, E, early_wait, 0)

    def scale_early(s, carry):
        for k in range(E):
            for b in range(B):
                value = (early[s, k, b] * factor).astype(jnp.bfloat16)
                for j in range(blocks):
                    scaled[s * B + b, j, k * C : (k + 1) * C] = value[:, j * LANES : (j + 1) * LANES]
        return carry

    lax.fori_loop(0, F, scale_early, 0)
    first = pltpu.make_async_copy(scaled, out.at[:, :, pl.ds(0, E * C)], o_own.at[1])
    first.start()

    def drain(k, carry):
        await_bytes(z_slots(k), z_send.at[k])
        spread(k, m, mx, x_send, x_recv).wait_send()
        spread(k, m, my, y_send, y_recv).wait_send()
        relay_y(k).wait_send()
        relay_x(k).wait_send()

        @pl.when(k < E)
        def _():
            await_bytes(early_slots(k), e_send.at[k])

        return carry

    lax.fori_loop(0, K, drain, 0)
    await_bytes(own_slots(m), ox_send)
    await_bytes(own_slots(m), oy_send)
    own_relay().wait_send()
    mine.wait()
    first.wait()
    await_bytes(ready.at[pl.ds(0, F - 1)], o_send)
    await_bytes(ready.at[pl.ds(0, F - 1)], o_recv)


def kernel_body(sources, mapping):
    F = lax.axis_size("freq")
    M = lax.axis_size("mode")
    bins, snaps = sources.shape[:2]
    B, _, O, modes = mapping.shape
    rows = 2 * snaps // F
    C = ROWS
    K = rows // C
    E = K * EARLY // 8
    blocks = O // LANES
    dma = pltpu.SemaphoreType.DMA
    any_space = pl.BlockSpec(memory_space=pl.ANY)
    out = pl.pallas_call(
        functools.partial(kernel, (F, M, B, K, C, O, E)),
        out_shape=jax.ShapeDtypeStruct((bins, blocks, rows, LANES), jnp.bfloat16),
        in_specs=[any_space, any_space],
        out_specs=any_space,
        scratch_shapes=[
            pltpu.VMEM((K, M, F, B, F, C, LANES), jnp.bfloat16),
            pltpu.VMEM((B, 2, O, modes), jnp.bfloat16),
            pltpu.VMEM((K, B, F, C, O), jnp.float32),
            pltpu.VMEM((F, E, B, C, O), jnp.float32),
            pltpu.VMEM((F, B, blocks, (K - E) * C, LANES), jnp.bfloat16),
            pltpu.VMEM((bins, blocks, E * C, LANES), jnp.bfloat16),
            pltpu.VMEM((8, LANES), jnp.float32),
            pltpu.VMEM((M, 8, LANES), jnp.float32),
            pltpu.VMEM((F, 8, LANES), jnp.float32),
            dma((B, 2)),
        ]
        + [dma((K,))] * 11
        + [dma((E,))] * 2
        + [dma(())] * 10
        + [dma((2,))]
        + [dma(())] * 2,
        compiler_params=pltpu.CompilerParams(
            collective_id=0, has_side_effects=True, vmem_limit_bytes=62 * 1024 * 1024
        ),
    )(sources.reshape(bins, F, rows, LANES), mapping)
    out = out.reshape(bins, blocks, rows // 2, 2, LANES)
    return jnp.transpose(out, (0, 2, 3, 1, 4)).reshape(bins, rows // 2, 2, O)


def body(sources, mapping):
    freq_count = lax.axis_size("freq")
    snaps, width = sources.shape[1], sources.shape[3]
    held = 2 * mapping.size + 2 * mapping.shape[0] * snaps * 2 * mapping.shape[3]
    fits = (
        lax.axis_size("mode") == 4
        and freq_count % 2 == 0
        and width == LANES
        and mapping.shape[2] % LANES == 0
        and snaps % (4 * ROWS * freq_count) == 0
        and held <= 40 * 1024 * 1024
    )
    return (kernel_body if fits else plain_body)(sources, mapping)


def solution(mesh):
    placed = (P(None, None, None, ("freq", "mode")), P("freq", None, "mode", None))
    return jax.shard_map(
        body, mesh=mesh, in_specs=placed, out_specs=P(None, "freq", None, "mode"), check_vma=False
    )
```
